256 devices in a mesh: tm: 16 (over x, y_lo, core), space: 16 (over y_hi, z).
Axes of the slice: x: 4, y: 4 (y_hi: 2, y_lo: 2; y = y_hi * 2 + y_lo), z: 8, core: 2. Of those that a mesh axis runs over, the one named last changes fastest.
Arguments:
- snapshots: bfloat16 [8192, 32768], P('tm', 'space'), may hold values from -6 to 6
- outlier_cols: int32 [64, 64], P('tm', 'space'), may hold values from 0 to 15
- outlier_values: bfloat16 [64, 64, 128, 128], P('tm', 'space'), may hold values from -12 to 12
- threshold: float32 [], replicated, may hold values from 0.3 to 0.9
Outputs:
- gram_band: float32 [8192, 9, 512], P('tm', None, 'space')
The draws below stay inside these ranges and needn't reach their ends.
Inputs may be any that keep to these rules, and one draw needn't show every extreme that they name: `outlier_cols`: entry k of a row lies in the points of space block k // 4; repeated entries add.
All inputs are finite; a program needn't handle non-finite values.
Results may differ from the reference program's by a relative error of at most 0.0021.
Values may be sent and summed in bfloat16 or wider, within the bound.
A program may use at most 128 MiB of HBM per device.

```python
import jax
import jax.numpy as jnp
from jax import lax

TB = 512
SP_DEV = 2048
OT = 128
ST = 128
KT = 4
TIME = 8192
SPACE = 32768
NH = 9
N_TM = 16
N_SPACE = 16


def plant(entries, own_key, least, high):
    longest = entries.shape.index(max(entries.shape))
    spots = []
    for shift in (0, 1):
        where = [jax.random.randint(jax.random.fold_in(own_key, axis), (), 0, length) for axis, length in enumerate(entries.shape)]
        where[longest] = (where[longest] + shift) % entries.shape[longest]
        spots.append(tuple(where))
    return entries.at[spots[0]].set(least).at[spots[1]].set(high)


def block_levels(own_key, shape, split, smallest, largest):
    def one(position, parts):
        draws = jax.random.uniform(jax.random.fold_in(jax.random.fold_in(own_key, 6), position), (parts,), jnp.float32, smallest / len(split), largest / len(split))
        return jnp.repeat(jnp.exp(draws), shape[position] // parts).reshape((-1,) + (1,) * (len(shape) - position - 1))

    loudness = one(*split[0])
    for cut in split[1:]:
        loudness = loudness * one(*cut)
    return loudness


def noise(stream_key, shape, deviation, most, split=(), held_as=jnp.bfloat16):
    values = jax.random.normal(stream_key, shape, jnp.float32) * deviation
    if len(split) > 0:
        values = block_levels(stream_key, shape, split, -0.22, 0.18) * values
    return jnp.clip(values, min=-most, max=most).astype(held_as)


def setup_inputs(seed: int = 0) -> dict:
    key_list = jax.random.split(jax.random.key(seed), 5)
    snapshots = noise(key_list[0], (TIME, SPACE), 1.0, 6.0, ((0, 16), (1, 16)))
    outlier_cols = plant(jax.random.randint(key_list[1], (TIME // OT, N_SPACE * KT), 0, SP_DEV // ST), jax.random.fold_in(key_list[1], 1), 0, (SP_DEV // ST) - 1).astype(jnp.int32)
    outlier_values = noise(key_list[2], (TIME // OT, N_SPACE * KT, OT, ST), 3.0, 12.0, ((0, 16), (1, 16)))
    threshold = jnp.clip(jax.random.uniform(key_list[3], (), jnp.float32, 0.3, 0.9), 0.3, 0.9)
    return {"snapshots": snapshots, "outlier_cols": outlier_cols, "outlier_values": outlier_values, "threshold": threshold}


def reference(snapshots, outlier_cols, outlier_values, threshold):
    rows = TIME // OT
    tiles_dev = SP_DEV // ST
    cols = outlier_cols.reshape(rows, N_SPACE, KT) + (jnp.arange(N_SPACE, dtype=jnp.int32) * tiles_dev)[None, :, None]
    cols = cols.reshape(rows, N_SPACE * KT)
    onehot = (cols[:, :, None] == jnp.arange(SPACE // ST, dtype=jnp.int32)[None, None, :]).astype(jnp.float32)

    def clean_rows(items):
        snap_rows, hot, vals = items
        dense = jnp.einsum('kos,kn->ons', vals.astype(jnp.float32), hot).reshape(OT, SPACE)
        diff = snap_rows.astype(jnp.float32) - dense
        return (jnp.sign(diff) * jnp.maximum(jnp.abs(diff) - threshold, 0.0)).astype(jnp.bfloat16)
    cleaned = lax.map(clean_rows, (snapshots.reshape(rows, OT, SPACE), onehot, outlier_values))
    blocks = cleaned.reshape(N_TM, TB, SPACE)
    scale = 1.0 / jnp.sqrt(jnp.float32(SPACE))

    def band_row(index):
        own = lax.dynamic_index_in_dim(blocks, index, 0, keepdims=False)
        tiles = []
        for step in range(NH):
            other = lax.dynamic_index_in_dim(blocks, (index + step) % N_TM, 0, keepdims=False)
            tiles.append(lax.dot_general(own, other, (((1,), (1,)), ((), ())), preferred_element_type=jnp.float32))
        return jnp.stack(tiles, axis=1) * scale
    band = lax.map(band_row, jnp.arange(N_TM, dtype=jnp.int32))
    return band.reshape(TIME, NH, TB)
```

```python
import jax
import jax.numpy as jnp
from jax import lax
from jax.experimental import pallas as pl
from jax.experimental.pallas import tpu as pltpu
from jax.sharding import PartitionSpec as P

ST = 128
MESH = pl.DeviceIdType.MESH
NX, NZ = 4, 8
TILES = 9


def clean_block(snapshots, outlier_cols, outlier_values, threshold):
    block_rows, points = snapshots.shape
    tiles_dev = points // ST
    onehot = (
        outlier_cols[:, :, None] == jnp.arange(tiles_dev, dtype=jnp.int32)[None, None, :]
    ).astype(jnp.bfloat16)
    dense = jnp.einsum("rkos,rkn->rons", outlier_values, onehot, preferred_element_type=jnp.float32)
    dense = dense.reshape(block_rows, points)
    diff = snapshots.astype(jnp.float32) - dense
    return (jnp.sign(diff) * jnp.maximum(jnp.abs(diff) - threshold, 0.0)).astype(jnp.bfloat16)


def kernel(
    clean, out, held, across, passing, part, sent, got, sum_out, sum_in,
    local_sem, g_send, g_recv, r_send, r_recv, f_send, f_recv,
):
    rows = clean.shape[0]
    via_up = passing.shape[0]
    tm, space = lax.axis_index("tm"), lax.axis_index("space")
    core, y, x = tm % 2, (tm // 2) % 2, tm // 4
    z, half = space % NZ, space // NZ

    def device(x=x, y=y, core=core, half=half, z=z):
        return ((x * 2 + y) * 2 + core, half * NZ + z)

    twin = device(core=1 - core)
    beside = device(y=1 - y)
    x_up, x_down = device(x=(x + 1) % NX), device(x=(x + NX - 1) % NX)
    z_up, z_down = device(z=(z + 1) % NZ), device(z=(z + NZ - 1) % NZ)
    far_own, far_beside = device(half=1 - half), device(half=1 - half, y=1 - y)

    load = pltpu.make_async_copy(clean, held.at[core], local_sem)
    load.start()
    barrier = pltpu.get_barrier_semaphore()
    peers = (twin, beside, x_up, x_down, z_up, z_down, far_own, far_beside)
    for peer in peers:
        pl.semaphore_signal(barrier, inc=1, device_id=peer, device_id_type=MESH)
    pl.semaphore_wait(barrier, len(peers))
    load.wait()

    def remote(src, dst, send, recv, to):
        return pltpu.make_async_remote_copy(
            src_ref=src, dst_ref=dst, send_sem=send, recv_sem=recv, device_id=to, device_id_type=MESH
        )

    own = held.at[core]
    mid = via_up // 2
    low, high = pl.ds(0, mid), pl.ds(mid, via_up - mid)
    rest = pl.ds(via_up, rows - via_up)
    copies = [
        (own, held.at[core], twin),
        (own, across, beside),
        (own, held.at[2 + core], x_down),
        (own.at[low], passing.at[low], x_up),
        (own.at[high], passing.at[high], x_up),
        (passing.at[low], held.at[4 + core, low], x_up),
        (passing.at[high], held.at[4 + core, high], x_up),
        (held.at[2 + core, rest], held.at[4 + core, rest], x_down),
        (held.at[2 + core], held.at[2 + core], twin),
        (held.at[4 + core, low], held.at[4 + core, low], twin),
        (held.at[4 + core, high], held.at[4 + core, high], twin),
        (held.at[4 + core, rest], held.at[4 + core, rest], twin),
    ]
    copies = [
        remote(src, dst, g_send.at[n], g_recv.at[n], to) for n, (src, dst, to) in enumerate(copies)
    ]
    for n in range(5):
        copies[n].start()

    def product(place, block, rhs):
        @pl.loop(0, 2)
        def _(q):
            columns = pl.ds(pl.multiple_of(q * 256, 256), 256)
            value = lax.dot_general(
                held[block], rhs[columns, :], (((1,), (1,)), ((), ())), preferred_element_type=jnp.float32
            )
            part[place, :, :, :, columns] = value.reshape(2, NZ, 32, 256)

    ways = ((z_down, -1, 0), (z_up, 1, 1))

    def ring_copy(place, way, step):
        to, _, first = ways[way]
        src, dst = sent.at[place, way, step], got.at[place, way, step]
        if step == 0:
            src, dst = src.at[first], dst.at[first]
        return remote(src, dst, r_send.at[place, way, step], r_recv.at[place, way, step], to)

    def ring_step(place, step):
        for way in range(2):
            _, sign, first = ways[way]
            goal = (z + NZ + sign * (4 - step)) % NZ
            if step > 0:
                ring_copy(place, way, step - 1).wait_recv()
            for h in range(2):
                if step == 0 and h != first:
                    continue
                value = part[place, h, goal]
                if step > 1 or (step == 1 and h == first):
                    value = value + got[place, way, step - 1, h].astype(jnp.float32)
                sent[place, way, step, h] = value.astype(jnp.bfloat16)
            ring_copy(place, way, step).start()

    def is_own(place):
        return place in (0, 1, 2, 7, 8)

    def final_copies(place):
        if is_own(place):
            return [remote(sum_out.at[place, 1 - half], sum_in.at[place, 0], f_send.at[place, 0], f_recv.at[place, 0], far_own)]
        return [
            remote(sum_out.at[place, half], sum_in.at[place, 0], f_send.at[place, 0], f_recv.at[place, 0], beside),
            remote(sum_out.at[place, 1 - half], sum_in.at[place, 1], f_send.at[place, 1], f_recv.at[place, 1], far_beside),
        ]

    def finish(place):
        for way in range(2):
            ring_copy(place, way, 3).wait_recv()
        for h in range(2):
            sum_out[place, h] = (
                part[place, h, z]
                + got[place, 0, 3, h].astype(jnp.float32)
                + got[place, 1, 3, h].astype(jnp.float32)
            )
        for copy in final_copies(place):
            copy.start()

    own_index = (0, 1, 2, None, None, None, None, 3, 4)

    def block_of(place):
        if is_own(place):
            return own_index[place] + core
        if place in (3, 4):
            return 2 + (place - 3)
        return 4 * (1 - y) + (place - 5)

    def distance(place):
        if is_own(place):
            block = block_of(place)
            return 4 * (block // 2) + block % 2 - core
        if place in (3, 4):
            return 2 + 4 * (1 - y) + (place - 3) - core
        return 2 + 4 * y + (place - 5) - core

    def put(place):
        for copy in final_copies(place):
            copy.wait_recv()
        if is_own(place):
            total = sum_out[place, half] + sum_in[place, 0]
        else:
            total = sum_in[place, 0] + sum_in[place, 1]
        out[distance(place)] = total

    def tick(now):
        for step in (3, 2, 1):
            if 0 <= now - step < TILES:
                ring_step(now - step, step)
        if 0 <= now - 4 < TILES:
            finish(now - 4)
        if 0 <= now - 6 < TILES:
            put(now - 6)

    for now in range(TILES + 6):
        if now == 1:
            copies[0].wait_recv()
            for n in (3, 4):
                copies[n].wait_recv()
                copies[n + 2].start()
            copies[2].wait_recv()
            copies[7].start()
            copies[8].start()
            copies[8].wait_recv()
            copies[1].wait_recv()
        if now == 5:
            for n in (5, 6, 7):
                copies[n].wait_recv()
                copies[n + 4 if n < 7 else 11].start()
            for n in (9, 10, 11):
                copies[n].wait_recv()
        if now < TILES:
            product(now, block_of(now), own if is_own(now) else across)
            ring_step(now, 0)
        tick(now)

    for copy in copies:
        copy.wait_send()
    for place in range(TILES):
        for way in range(2):
            for step in range(4):
                ring_copy(place, way, step).wait_send()
        for copy in final_copies(place):
            copy.wait_send()


def local(snapshots, outlier_cols, outlier_values, threshold):
    rows, points = snapshots.shape
    cleaned = clean_block(snapshots, outlier_cols, outlier_values, threshold)
    scale = 1.0 / jnp.sqrt(jnp.float32(points * lax.axis_size("space")))
    via_up = rows * 5 // 8
    piece = rows // (2 * NZ)
    band = pl.pallas_call(
        kernel,
        out_shape=jax.ShapeDtypeStruct((TILES, piece, rows), jnp.float32),
        in_specs=[pl.BlockSpec(memory_space=pl.ANY)],
        out_specs=pl.BlockSpec(memory_space=pltpu.VMEM),
        scratch_shapes=[
            pltpu.VMEM((6, rows, points), jnp.bfloat16),
            pltpu.VMEM((rows, points), jnp.bfloat16),
            pltpu.VMEM((via_up, points), jnp.bfloat16),
            pltpu.VMEM((TILES, 2, NZ, piece, rows), jnp.float32),
            pltpu.VMEM((TILES, 2, 4, 2, piece, rows), jnp.bfloat16),
            pltpu.VMEM((TILES, 2, 4, 2, piece, rows), jnp.bfloat16),
            pltpu.VMEM((TILES, 2, piece, rows), jnp.float32),
            pltpu.VMEM((TILES, 2, piece, rows), jnp.float32),
            pltpu.SemaphoreType.DMA,
            pltpu.SemaphoreType.DMA((12,)),
            pltpu.SemaphoreType.DMA((12,)),
            pltpu.SemaphoreType.DMA((TILES, 2, 4)),
            pltpu.SemaphoreType.DMA((TILES, 2, 4)),
            pltpu.SemaphoreType.DMA((TILES, 2)),
            pltpu.SemaphoreType.DMA((TILES, 2)),
        ],
        compiler_params=pltpu.CompilerParams(
            collective_id=0, has_side_effects=True, vmem_limit_bytes=62 * 1024 * 1024
        ),
    )(cleaned)
    return jnp.transpose(band, (2, 0, 1)) * scale


def solution(mesh):
    placed = (P("tm", "space"), P("tm", "space"), P("tm", "space", None, None), P())
    return jax.shard_map(
        local, mesh=mesh, in_specs=placed, out_specs=P("tm", None, "space"), check_vma=False
    )
```

```python
import jax
import jax.numpy as jnp
from jax import lax
from jax.experimental import pallas as pl
from jax.experimental.pallas import tpu as pltpu
from jax.sharding import PartitionSpec as P

MESH = pl.DeviceIdType.MESH
NX, NZ = 4, 8
PARTS = 4
UNITS = 18
DRAINS = (2, 2, 1, 1, 0, 0)


def kernel(
    cols, threshold, snapshots, values, out,
    held, natural, before, part, sent, got, sum_out, sum_in,
    a_send, a_recv, b_send, b_recv, e_send, e_recv, h_send, h_recv,
    tb_send, tb_recv, th_send, th_recv, r_send, r_recv, f_send, f_recv,
):
    rows, points = snapshots.shape
    size = rows // PARTS
    wide = rows // 2
    tm, space = lax.axis_index("tm"), lax.axis_index("space")
    core, y, x = tm % 2, (tm // 2) % 2, tm // 4
    z, half = space % NZ, space // NZ

    def device(x=x, y=y, core=core, half=half, z=z):
        return ((x * 2 + y) * 2 + core, half * NZ + z)

    x_next, x_last = (x + 1) % NX, (x + NX - 1) % NX
    twin = device(core=1 - core)
    beside = device(y=1 - y)
    x_up, x_down = device(x=x_next), device(x=x_last)
    z_up, z_down = device(z=(z + 1) % NZ), device(z=(z + NZ - 1) % NZ)
    far, far_up, far_down = device(half=1 - half), device(x=x_next, half=1 - half), device(x=x_last, half=1 - half)

    barrier = pltpu.get_barrier_semaphore()
    peers = (twin, beside, x_up, x_down, z_up, z_down, far, far_up, far_down)
    for peer in peers:
        pl.semaphore_signal(barrier, inc=1, device_id=peer, device_id_type=MESH)

    tile_rows, tile_points = values.shape[2:]
    limit = threshold[0, 0]

    @pl.loop(0, points // tile_points)
    def _(c):
        lanes = pl.ds(pl.multiple_of(c * tile_points, tile_points), tile_points)
        for r in range(rows // tile_rows):
            across = pl.ds(r * tile_rows, tile_rows)
            dense = jnp.zeros((tile_rows, tile_points), jnp.float32)
            for k in range(values.shape[1]):
                listed = (cols[r, k] == c).astype(jnp.float32)
                dense = dense + listed * values[r, k].astype(jnp.float32)
            diff = snapshots[across, lanes].astype(jnp.float32) - dense
            shrunk = diff - jnp.clip(diff, -limit, limit)
            natural[across, lanes] = shrunk.astype(jnp.bfloat16)
            groups = shrunk.reshape(tile_rows // 32, PARTS, 8, tile_points)
            for n in range(PARTS):
                piece = groups[:, n].reshape(tile_rows // PARTS, tile_points)
                held[core, pl.ds(n * size + r * (tile_rows // PARTS), tile_rows // PARTS), lanes] = piece.astype(jnp.bfloat16)

    pl.semaphore_wait(barrier, len(peers))

    def remote(src, dst, send, recv, to):
        return pltpu.make_async_remote_copy(
            src_ref=src, dst_ref=dst, send_sem=send, recv_sem=recv, device_id=to, device_id_type=MESH
        )

    def portion(block, n):
        return held.at[block, pl.ds(n * size, size)]

    a_copy = [remote(portion(core, n), portion(core, n), a_send.at[n], a_recv.at[n], twin) for n in range(PARTS)]
    b_copy = [remote(portion(core, n), portion(2 + core, n), b_send.at[n], b_recv.at[n], x_down) for n in range(PARTS)]
    e_copy = [
        remote(natural.at[pl.ds(q * wide, wide)], before.at[pl.ds(q * wide, wide)], e_send.at[q], e_recv.at[q], x_up)
        for q in range(2)
    ]
    h_from = core + 2 * (1 - y)
    h_copy = [remote(portion(h_from, n), portion(4 + core, n), h_send.at[n], h_recv.at[n], beside) for n in range(PARTS)]
    tb_copy = [remote(portion(2 + core, n), portion(2 + core, n), tb_send.at[n], tb_recv.at[n], twin) for n in range(PARTS)]
    th_copy = [remote(portion(4 + core, n), portion(4 + core, n), th_send.at[n], th_recv.at[n], twin) for n in range(PARTS)]
    gathers = a_copy + b_copy + e_copy + h_copy + tb_copy + th_copy
    for copy in a_copy[:1] + b_copy[:1] + e_copy[:1] + a_copy[1:] + b_copy[1:] + e_copy[1:]:
        copy.start()

    def aa(n):
        return ("a", 0, (core, 1), (n * (1 + core), n * (1 + core) + core))

    def ab(n):
        return ("a", 4, (2, 3), (n, n))

    def ah(n):
        return ("a", 2, (4, 5), (n, n))

    def eh(q, n):
        return ("e", 6, (4, 5), (n, n), q)

    def eb(q, n):
        return ("e", 8, (2, 3), (n, n), q)

    def eb_last(q):
        return ("e", 8, (2, 2 + core), (core, 1), q)

    rounds = (
        ((aa(0),), (aa(1),)),
        ((ab(0),),),
        ((ab(1),), (ah(0),), (aa(2), eb(0, 0))),
        ((ab(2),), (ah(1),), (eh(0, 0),)),
        ((ab(3),), (ah(2),), (aa(3), eb(1, 0)), (eb_last(0),), (eb_last(1),), (eh(1, 0),)),
        ((ah(3),), (eh(0, 1),), (eh(1, 1),)),
    )
    units = [unit for group in rounds for unit in group]

    def each(place, action):
        if len(units[place]) == 1:
            action(units[place][0])
        else:
            for n, unit in enumerate(units[place]):
                @pl.when(core == n)
                def _(unit=unit):
                    action(unit)

    def rows_of(block, n, count):
        return held[block, pl.ds(pl.multiple_of(n * count, count), count), :]

    def times(left, right):
        return lax.dot_general(left, right, (((1,), (1,)), ((), ())), preferred_element_type=jnp.float32)

    def product(place):
        def action(unit):
            kind, _, blocks, parts = unit[:4]
            if kind == "a":
                left = jnp.concatenate([rows_of(b, n, size) for b, n in zip(blocks, parts)], axis=0)

                @pl.loop(0, 2)
                def _(q):
                    columns = pl.ds(pl.multiple_of(q * wide, wide), wide)
                    value = times(left, natural[columns, :]).reshape(2, 2, NZ, 8, wide)
                    for i in range(2):
                        part[place, :, :, pl.ds(8 * i, 8), columns] = value[i]
            else:
                q = unit[4]
                right = before[pl.ds(q * wide, wide), :]
                for i, (b, n) in enumerate(zip(blocks, parts)):
                    value = times(rows_of(b, n, 2 * size), right).reshape(2, 2, NZ, 8, wide)
                    for j in range(2):
                        part[place, :, :, pl.ds(8 * j, 8), pl.ds(i * wide, wide)] = value[j]

        each(place, action)

    ways = ((z_down, -1, 0), (z_up, 1, 1))

    def ring_copy(place, way, step):
        to, _, first = ways[way]
        src, dst = sent.at[place, way, step], got.at[place, way, step]
        if step == 0:
            src, dst = src.at[first], dst.at[first]
        return remote(src, dst, r_send.at[place, way, step], r_recv.at[place, way, step], to)

    def ring_step(place, step):
        for way in range(2):
            _, sign, first = ways[way]
            goal = (z + NZ + sign * (4 - step)) % NZ
            if step > 0:
                ring_copy(place, way, step - 1).wait_recv()
            for h in range(2):
                if step == 0 and h != first:
                    continue
                value = part[place, h, goal]
                if step > 1 or (step == 1 and h == first):
                    value = value + got[place, way, step - 1, h].astype(jnp.float32)
                sent[place, way, step, h] = value.astype(jnp.bfloat16)
            ring_copy(place, way, step).start()

    def final_copies(place, unit):
        def copy(h, n, to):
            return remote(sum_out.at[place, h], sum_in.at[place, n], f_send.at[place, n], f_recv.at[place, n], to)

        if unit[0] == "a":
            return [copy(1 - half, 0, far)]
        return [copy(half, 0, x_down), copy(1 - half, 1, far_down)]

    def finish(place):
        for way in range(2):
            ring_copy(place, way, 3).wait_recv()
        for h in range(2):
            sum_out[place, h] = (
                part[place, h, z]
                + got[place, 0, 3, h].astype(jnp.float32)
                + got[place, 1, 3, h].astype(jnp.float32)
            )

        def action(unit):
            for copy in final_copies(place, unit):
                copy.start()

        each(place, action)

    def put(place):
        def action(unit):
            kind, base, blocks, parts = unit[:4]
            for copy in final_copies(place, unit):
                copy.wait_recv()
            if kind == "a":
                total = sum_out[place, half] + sum_in[place, 0]
            else:
                total = sum_in[place, 0] + sum_in[place, 1]
            for i, (b, n) in enumerate(zip(blocks, parts)):
                k = base + b % 2 - core
                if kind == "a":
                    out[k, pl.ds(pl.multiple_of(8 * n, 8), 8), :] = total[8 * i : 8 * i + 8]
                else:
                    q = unit[4]
                    out[k, pl.ds(pl.multiple_of(16 * n, 16), 16), pl.ds(q * wide, wide)] = total[:, i * wide : (i + 1) * wide]

        each(place, action)

    flying = []

    def advance():
        for entry in list(flying):
            place, stage = entry
            if stage < 4:
                ring_step(place, stage)
            elif stage == 4:
                finish(place)
            elif stage == 6:
                put(place)
                flying.remove(entry)
                continue
            entry[1] += 1

    def arrive(number):
        if number == 0:
            a_copy[0].wait_recv()
            a_copy[1].wait_recv()
            return
        if number <= PARTS:
            b_copy[number - 1].wait_recv()
            h_copy[number - 1].start()
            tb_copy[number - 1].start()
        if number >= 2:
            h_copy[number - 2].wait_recv()
            th_copy[number - 2].start()
        if number == 2:
            a_copy[2].wait_recv()
            a_copy[3].wait_recv()
            e_copy[0].wait_recv()
        if number == 4:
            e_copy[1].wait_recv()
        if number <= PARTS:
            tb_copy[number - 1].wait_recv()
        if number >= 2:
            th_copy[number - 2].wait_recv()

    place = 0
    for number, group in enumerate(rounds):
        arrive(number)
        for _ in group:
            advance()
            product(place)
            ring_step(place, 0)
            flying.append([place, 1])
            place += 1
        for _ in range(DRAINS[number]):
            advance()
    while flying:
        advance()

    for copy in gathers:
        copy.wait_send()
    for place in range(UNITS):
        for way in range(2):
            for step in range(4):
                ring_copy(place, way, step).wait_send()

        def sent_all(unit, place=place):
            for copy in final_copies(place, unit):
                copy.wait_send()

        each(place, sent_all)


def local(snapshots, outlier_cols, outlier_values, threshold):
    rows, points = snapshots.shape
    scale = 1.0 / jnp.sqrt(jnp.float32(points * lax.axis_size("space")))
    dma = pltpu.SemaphoreType.DMA
    pairs = [PARTS, PARTS, 2, PARTS, PARTS, PARTS]
    band = pl.pallas_call(
        kernel,
        out_shape=jax.ShapeDtypeStruct((9, 32, rows), jnp.float32),
        in_specs=[pl.BlockSpec(memory_space=pltpu.SMEM)] * 2 + [pl.BlockSpec(memory_space=pltpu.VMEM)] * 2,
        out_specs=pl.BlockSpec(memory_space=pltpu.VMEM),
        scratch_shapes=[
            pltpu.VMEM((6, rows, points), jnp.bfloat16),
            pltpu.VMEM((rows, points), jnp.bfloat16),
            pltpu.VMEM((rows, points), jnp.bfloat16),
            pltpu.VMEM((UNITS, 2, NZ, 16, rows), jnp.float32),
            pltpu.VMEM((UNITS, 2, 4, 2, 16, rows), jnp.bfloat16),
            pltpu.VMEM((UNITS, 2, 4, 2, 16, rows), jnp.bfloat16),
            pltpu.VMEM((UNITS, 2, 16, rows), jnp.float32),
            pltpu.VMEM((UNITS, 2, 16, rows), jnp.float32),
            *[dma((n,)) for count in pairs for n in (count, count)],
            dma((UNITS, 2, 4)),
            dma((UNITS, 2, 4)),
            dma((UNITS, 2)),
            dma((UNITS, 2)),
        ],
        compiler_params=pltpu.CompilerParams(
            collective_id=0, has_side_effects=True, vmem_limit_bytes=58 * 1024 * 1024
        ),
    )(outlier_cols, threshold.reshape(1, 1), snapshots, outlier_values)
    return jnp.transpose(band, (2, 0, 1)) * scale


def solution(mesh):
    placed = (P("tm", "space"), P("tm", "space"), P("tm", "space", None, None), P())
    return jax.shard_map(
        local, mesh=mesh, in_specs=placed, out_specs=P("tm", None, "space"), check_vma=False
    )
```

```python
import jax
import jax.numpy as jnp
from jax import lax
from jax.experimental import pallas as pl
from jax.experimental.pallas import tpu as pltpu
from jax.sharding import PartitionSpec as P

MESH = pl.DeviceIdType.MESH
NX, NZ = 4, 8
PARTS, PIECES = 4, 8
UNITS = 18

NEEDS = (
    (("a", 1),), (("a", 2),),
    (("b", 1),),
    (("b", 2),), (("h", 1),), (("a", 3), ("b", 2), ("e", 1)),
    (("b", 3),), (("h", 2),), (("h", 2), ("e", 1)),
    (("b", 4),), (("h", 3),), (("a", 4), ("b", 2), ("e", 2)),
    (("b", 4), ("e", 1)), (("b", 4), ("e", 2)), (("h", 2), ("e", 2)),
    (("h", 4), ("e", 1)), (("h", 4), ("e", 2)), (("h", 4),),
)


def plan():
    rate, twin_rate, hop, twin_hop, multiply, add = 45.0, 220.0, 2.0, 1.0, 0.85, 0.12
    free, there, now, order = {}, {}, 0.0, []

    def send(link, size, latency=hop, speed=rate):
        free[link] = max(now, free.get(link, 0.0)) + size / speed
        return free[link] + latency

    piece = 2048 / PIECES
    for n in range(PIECES):
        there["a", n] = send("twin", piece, twin_hop, twin_rate)
        there["b", n] = send("down", piece)
    for n in range(2):
        there["e", n] = send("up", 1024)
    waiting = [(kind, n) for kind in "bh" for n in range(PIECES)]
    todo, flying = list(range(UNITS)), {}
    passed = {"a": "a", "b": "tb", "h": "th"}
    while todo or flying:
        choice = []
        for kind in "bh":
            left = [n for k, n in waiting if k == kind]
            if left and (kind, left[0]) in there:
                choice.append((there[kind, left[0]], 0, left[0], 0, (kind, left[0])))
        for unit in todo:
            keys = [
                (passed.get(k, k), n)
                for k, count in NEEDS[unit]
                for n in range(count * (1 if k == "e" else PIECES // PARTS))
            ]
            if all(key in there for key in keys):
                choice.append((max(there[key] for key in keys), 2, unit, 0, ("unit", unit)))
        for unit, at in flying.items():
            for way in range(2):
                step = at[way]
                if step < 4:
                    choice.append((at[way, step - 1], 1, unit, step, ("hop", unit, way, step)))
            if "sum" in at:
                choice.append((at["sum"], 3, unit, 5, ("put", unit)))
            elif at[0] == at[1] == 4:
                choice.append((max(at[0, 3], at[1, 3]), 1, unit, 4, ("sum", unit)))
        now = max(now, min(c[0] for c in choice))
        action = min((c for c in choice if c[0] <= now), key=lambda c: c[1:4])[4]
        order.append(action)
        kind, n = action[:2]
        if kind == "b":
            waiting.remove(action)
            there["h", n] = send("beside", piece)
            there["tb", n] = send("twin", piece, twin_hop, twin_rate)
        elif kind == "h":
            waiting.remove(action)
            there["th", n] = send("twin", piece, twin_hop, twin_rate)
        elif kind == "unit":
            todo.remove(n)
            now += multiply + add
            flying[n] = {way: 1 for way in range(2)}
            for way in range(2):
                flying[n][way, 0] = send(way, 16)
        elif kind == "hop":
            way, step = action[2:]
            now += add
            flying[n][way, step] = send(way, 32)
            flying[n][way] = step + 1
        elif kind == "sum":
            now += add
            flying[n]["sum"] = send("far", 40, hop + 1.5)
        else:
            now += add
            del flying[n]
    return order


def kernel(
    cols, threshold, snapshots_in, values_in, out,
    snapshots, values, held, natural, before, part, sent, got, sum_out, sum_in,
    in_sem, g_send, a_recv, b_recv, e_recv, h_recv, tb_recv, th_recv,
    first_send, r_send, r_recv, f_send, f_recv,
):
    rows, points = snapshots.shape
    size = rows // PARTS
    wide = rows // 2
    tm, space = lax.axis_index("tm"), lax.axis_index("space")
    core, y, x = tm % 2, (tm // 2) % 2, tm // 4
    z, half = space % NZ, space // NZ

    def device(x=x, y=y, core=core, half=half, z=z):
        return ((x * 2 + y) * 2 + core, half * NZ + z)

    x_next, x_last = (x + 1) % NX, (x + NX - 1) % NX
    twin = device(core=1 - core)
    beside = device(y=1 - y)
    x_up, x_down = device(x=x_next), device(x=x_last)
    z_up, z_down = device(z=(z + 1) % NZ), device(z=(z + NZ - 1) % NZ)
    far, far_up, far_down = device(half=1 - half), device(x=x_next, half=1 - half), device(x=x_last, half=1 - half)

    barrier = pltpu.get_barrier_semaphore()
    peers = (twin, beside, x_up, x_down, z_up, z_down, far, far_up, far_down)
    for peer in peers:
        pl.semaphore_signal(barrier, inc=1, device_id=peer, device_id_type=MESH)
    loads = [
        pltpu.make_async_copy(values_in, values, in_sem.at[0]),
        pltpu.make_async_copy(snapshots_in, snapshots, in_sem.at[1]),
    ]
    for load in loads:
        load.start()
    for load in loads:
        load.wait()

    tile_rows, tile_points = values.shape[2:]
    limit = threshold[0, 0]

    @pl.loop(0, points // tile_points)
    def _(c):
        lanes = pl.ds(pl.multiple_of(c * tile_points, tile_points), tile_points)
        for r in range(rows // tile_rows):
            across = pl.ds(r * tile_rows, tile_rows)
            dense = jnp.zeros((tile_rows, tile_points), jnp.float32)
            for k in range(values.shape[1]):
                listed = (cols[r, k] == c).astype(jnp.float32)
                dense = dense + listed * values[r, k].astype(jnp.float32)
            diff = snapshots[across, lanes].astype(jnp.float32) - dense
            shrunk = diff - jnp.clip(diff, -limit, limit)
            natural[across, lanes] = shrunk.astype(jnp.bfloat16)
            groups = shrunk.reshape(tile_rows // 32, PARTS, 8, tile_points)
            for n in range(PARTS):
                piece = groups[:, n].reshape(tile_rows // PARTS, tile_points)
                held[core, pl.ds(n * size + r * (tile_rows // PARTS), tile_rows // PARTS), lanes] = piece.astype(jnp.bfloat16)

    pl.semaphore_wait(barrier, len(peers))

    def remote(src, dst, send, recv, to):
        return pltpu.make_async_remote_copy(
            src_ref=src, dst_ref=dst, send_sem=send, recv_sem=recv, device_id=to, device_id_type=MESH
        )

    def portion(block, n):
        return held.at[block, pl.ds(n * (rows // PIECES), rows // PIECES)]

    a_copy = [remote(portion(core, n), portion(core, n), g_send, a_recv.at[n], twin) for n in range(PIECES)]
    b_copy = [remote(portion(core, n), portion(2 + core, n), g_send, b_recv.at[n], x_down) for n in range(PIECES)]
    e_copy = [
        remote(natural.at[pl.ds(q * wide, wide)], before.at[pl.ds(q * wide, wide)], g_send, e_recv.at[q], x_up)
        for q in range(2)
    ]
    h_from = core + 2 * (1 - y)
    h_copy = [remote(portion(h_from, n), portion(4 + core, n), g_send, h_recv.at[n], beside) for n in range(PIECES)]
    tb_copy = [remote(portion(2 + core, n), portion(2 + core, n), g_send, tb_recv.at[n], twin) for n in range(PIECES)]
    th_copy = [remote(portion(4 + core, n), portion(4 + core, n), g_send, th_recv.at[n], twin) for n in range(PIECES)]
    for copy in a_copy[:1] + b_copy[:1] + e_copy[:1] + a_copy[1:] + b_copy[1:] + e_copy[1:]:
        copy.start()

    def aa(n):
        return ("a", 0, (core, 1), (n * (1 + core), n * (1 + core) + core))

    def ab(n):
        return ("a", 4, (2, 3), (n, n))

    def ah(n):
        return ("a", 2, (4, 5), (n, n))

    def eh(q, n):
        return ("e", 6, (4, 5), (n, n), q)

    def eb(q, n):
        return ("e", 8, (2, 3), (n, n), q)

    def eb_last(q):
        return ("e", 8, (2, 2 + core), (core, 1), q)

    rounds = (
        ((aa(0),), (aa(1),)),
        ((ab(0),),),
        ((ab(1),), (ah(0),), (aa(2), eb(0, 0))),
        ((ab(2),), (ah(1),), (eh(0, 0),)),
        ((ab(3),), (ah(2),), (aa(3), eb(1, 0)), (eb_last(0),), (eb_last(1),), (eh(1, 0),)),
        ((eh(0, 1),), (eh(1, 1),), (ah(3),)),
    )
    units = [unit for group in rounds for unit in group]

    def each(place, action):
        if len(units[place]) == 1:
            action(units[place][0])
        else:
            for n, unit in enumerate(units[place]):
                @pl.when(core == n)
                def _(unit=unit):
                    action(unit)

    def rows_of(block, n, count):
        return held[block, pl.ds(pl.multiple_of(n * count, count), count), :]

    def times(left, right):
        return lax.dot_general(left, right, (((1,), (1,)), ((), ())), preferred_element_type=jnp.float32)

    def product(place):
        def action(unit):
            kind, _, blocks, parts = unit[:4]
            if kind == "a":
                left = jnp.concatenate([rows_of(b, n, size) for b, n in zip(blocks, parts)], axis=0)

                @pl.loop(0, 2)
                def _(q):
                    columns = pl.ds(pl.multiple_of(q * wide, wide), wide)
                    value = times(left, natural[columns, :]).reshape(2, 2, NZ, 8, wide)
                    for i in range(2):
                        part[place, :, :, pl.ds(8 * i, 8), columns] = value[i]
            else:
                q = unit[4]
                right = before[pl.ds(q * wide, wide), :]
                for i, (b, n) in enumerate(zip(blocks, parts)):
                    value = times(rows_of(b, n, 2 * size), right).reshape(2, 2, NZ, 8, wide)
                    for j in range(2):
                        part[place, :, :, pl.ds(8 * j, 8), pl.ds(i * wide, wide)] = value[j]

        each(place, action)

    ways = ((z_down, -1, 0), (z_up, 1, 1))

    def ring_copy(place, way, step):
        to, _, first = ways[way]
        src, dst = sent.at[place, way, step], got.at[place, way, step]
        if step == 0:
            src, dst = src.at[first], dst.at[first]
        return remote(src, dst, r_send if step else first_send, r_recv.at[place, way, step], to)

    def hop(place, way, step):
        _, sign, first = ways[way]
        goal = (z + NZ + sign * (4 - step)) % NZ
        if step > 0:
            ring_copy(place, way, step - 1).wait_recv()
        for h in range(2):
            if step == 0 and h != first:
                continue
            value = part[place, h, goal]
            if step > 1 or (step == 1 and h == first):
                value = value + got[place, way, step - 1, h].astype(jnp.float32)
            sent[place, way, step, h] = value.astype(jnp.bfloat16)
        ring_copy(place, way, step).start()

    def final_copies(place, unit):
        def copy(h, n, to):
            return remote(sum_out.at[place, h], sum_in.at[place, n], f_send.at[place, n], f_recv.at[place, n], to)

        if unit[0] == "a":
            return [copy(1 - half, 0, far)]
        return [copy(half, 0, x_down), copy(1 - half, 1, far_down)]

    def finish(place):
        for way in range(2):
            ring_copy(place, way, 3).wait_recv()
        for h in range(2):
            sum_out[place, h] = (
                part[place, h, z]
                + got[place, 0, 3, h].astype(jnp.float32)
                + got[place, 1, 3, h].astype(jnp.float32)
            )

        def action(unit):
            for copy in final_copies(place, unit):
                copy.start()

        each(place, action)

    def put(place):
        def action(unit):
            kind, base, blocks, parts = unit[:4]
            for copy in final_copies(place, unit):
                copy.wait_recv()
            if kind == "a":
                total = sum_out[place, half] + sum_in[place, 0]
            else:
                total = sum_in[place, 0] + sum_in[place, 1]
            for i, (b, n) in enumerate(zip(blocks, parts)):
                k = base + b % 2 - core
                if kind == "a":
                    out[k, pl.ds(pl.multiple_of(8 * n, 8), 8), :] = total[8 * i : 8 * i + 8]
                else:
                    q = unit[4]
                    out[k, pl.ds(pl.multiple_of(16 * n, 16), 16), pl.ds(q * wide, wide)] = total[:, i * wide : (i + 1) * wide]

        each(place, action)

    copies = {"a": a_copy, "b": tb_copy, "h": th_copy, "e": e_copy}
    waited = {kind: 0 for kind in copies}

    def need(kind, count):
        count *= 1 if kind == "e" else PIECES // PARTS
        for n in range(waited[kind], count):
            copies[kind][n].wait_recv()
        waited[kind] = max(waited[kind], count)

    for kind, n, *rest in plan():
        if kind == "b":
            b_copy[n].wait_recv()
            h_copy[n].start()
            tb_copy[n].start()
        elif kind == "h":
            h_copy[n].wait_recv()
            th_copy[n].start()
        elif kind == "unit":
            for what, count in NEEDS[n]:
                need(what, count)
            product(n)
            for way in range(2):
                hop(n, way, 0)
        elif kind == "hop":
            hop(n, *rest)
        elif kind == "sum":
            finish(n)
        else:
            put(n)

    remote(held, held, g_send, a_recv.at[0], twin).wait_send()
    steps = sent.at[:, :, pl.ds(1, 3)]
    remote(steps, steps, r_send, a_recv.at[0], twin).wait_send()
    firsts = sent.at[:, :, 0, 0]
    remote(firsts, firsts, first_send, a_recv.at[0], twin).wait_send()
    for place in range(UNITS):
        def sent_all(unit, place=place):
            for copy in final_copies(place, unit):
                copy.wait_send()

        each(place, sent_all)


def local(snapshots, outlier_cols, outlier_values, threshold):
    rows, points = snapshots.shape
    scale = 1.0 / jnp.sqrt(jnp.float32(points * lax.axis_size("space")))
    dma = pltpu.SemaphoreType.DMA
    band = pl.pallas_call(
        kernel,
        out_shape=jax.ShapeDtypeStruct((9, 32, rows), jnp.float32),
        in_specs=[pl.BlockSpec(memory_space=pltpu.SMEM)] * 2 + [pl.BlockSpec(memory_space=pl.ANY)] * 2,
        out_specs=pl.BlockSpec(memory_space=pltpu.VMEM),
        scratch_shapes=[
            pltpu.VMEM(snapshots.shape, jnp.bfloat16),
            pltpu.VMEM(outlier_values.shape, jnp.bfloat16),
            pltpu.VMEM((6, rows, points), jnp.bfloat16),
            pltpu.VMEM((rows, points), jnp.bfloat16),
            pltpu.VMEM((rows, points), jnp.bfloat16),
            pltpu.VMEM((UNITS, 2, NZ, 16, rows), jnp.float32),
            pltpu.VMEM((UNITS, 2, 4, 2, 16, rows), jnp.bfloat16),
            pltpu.VMEM((UNITS, 2, 4, 2, 16, rows), jnp.bfloat16),
            pltpu.VMEM((UNITS, 2, 16, rows), jnp.float32),
            pltpu.VMEM((UNITS, 2, 16, rows), jnp.float32),
            dma((2,)),
            dma,
            *[dma((count,)) for count in (PIECES, PIECES, 2, PIECES, PIECES, PIECES)],
            dma,
            dma,
            dma((UNITS, 2, 4)),
            dma((UNITS, 2)),
            dma((UNITS, 2)),
        ],
        compiler_params=pltpu.CompilerParams(
            collective_id=0, has_side_effects=True, vmem_limit_bytes=58 * 1024 * 1024
        ),
    )(outlier_cols, threshold.reshape(1, 1), snapshots, outlier_values)
    return jnp.transpose(band, (2, 0, 1)) * scale


def solution(mesh):
    placed = (P("tm", "space"), P("tm", "space"), P("tm", "space", None, None), P())
    return jax.shard_map(
        local, mesh=mesh, in_specs=placed, out_specs=P("tm", None, "space"), check_vma=False
    )
```

```python
import jax
import jax.numpy as jnp
from jax import lax
from jax.experimental import pallas as pl
from jax.experimental.pallas import tpu as pltpu
from jax.sharding import PartitionSpec as P

MESH = pl.DeviceIdType.MESH
NX, NZ = 4, 8
PARTS, PIECES = 4, 16
UNITS = 18

NEEDS = (
    (("a", 1),), (("a", 2),),
    (("b", 1),),
    (("b", 2),), (("h", 1),), (("a", 3), ("b", 2), ("e", 1)),
    (("b", 3),), (("h", 2),), (("h", 2), ("e", 1)),
    (("b", 4),), (("h", 3),), (("a", 4), ("b", 2), ("e", 2)),
    (("b", 4), ("e", 1)), (("b", 4), ("e", 2)), (("h", 2), ("e", 2)),
    (("h", 4), ("e", 1)), (("h", 4), ("e", 2)), (("h", 4),),
)


def plan():
    rate, twin_rate, hop, twin_hop, multiply, add = 44.0, 220.0, 3.5, 2.0, 0.85, 0.15
    free, there, now, order = {}, {}, 0.0, []

    def send(link, size, latency=hop, speed=rate):
        free[link] = max(now, free.get(link, 0.0)) + size / speed
        return free[link] + latency

    piece = 2048 / PIECES
    for n in range(PIECES):
        there["a", n] = send("twin", piece, twin_hop, twin_rate)
        there["b", n] = send("down", piece)
    for n in range(2):
        there["e", n] = send("up", 1024)
    waiting = [(kind, n) for kind in "bh" for n in range(PIECES)]
    todo, flying = list(range(UNITS)), {}
    passed = {"a": "a", "b": "tb", "h": "th"}
    while todo or flying:
        choice = []
        for kind in "bh":
            left = [n for k, n in waiting if k == kind]
            if left and (kind, left[0]) in there:
                choice.append((there[kind, left[0]], 0, left[0], 0, (kind, left[0])))
        for unit in todo:
            keys = [
                (passed.get(k, k), n)
                for k, count in NEEDS[unit]
                for n in range(count * (1 if k == "e" else PIECES // PARTS))
            ]
            if all(key in there for key in keys):
                choice.append((max(there[key] for key in keys), 2, unit, 0, ("unit", unit)))
        for unit, at in flying.items():
            for way in range(2):
                step = at[way]
                if step < 4:
                    choice.append((at[way, step - 1], 1, unit, step, ("hop", unit, way, step)))
            if "sum" in at:
                choice.append((at["sum"], 3, unit, 5, ("put", unit)))
            elif at[0] == at[1] == 4:
                choice.append((max(at[0, 3], at[1, 3]), 1, unit, 4, ("sum", unit)))
        now = max(now, min(c[0] for c in choice))
        action = min((c for c in choice if c[0] <= now), key=lambda c: c[1:4])[4]
        order.append(action)
        kind, n = action[:2]
        if kind == "b":
            waiting.remove(action)
            there["h", n] = send("beside", piece)
            there["tb", n] = send("twin", piece, twin_hop, twin_rate)
        elif kind == "h":
            waiting.remove(action)
            there["th", n] = send("twin", piece, twin_hop, twin_rate)
        elif kind == "unit":
            todo.remove(n)
            now += multiply + add
            flying[n] = {way: 1 for way in range(2)}
            for way in range(2):
                flying[n][way, 0] = send(way, 16)
        elif kind == "hop":
            way, step = action[2:]
            now += add
            flying[n][way, step] = send(way, 32)
            flying[n][way] = step + 1
        elif kind == "sum":
            now += add
            flying[n]["sum"] = send("far", 40, hop + 1.5)
        else:
            now += add
            del flying[n]
    return order


def kernel(
    cols, threshold, snapshots_in, values_in, out,
    snapshots, values, held, natural, before, part, sent, got, sum_out, sum_in,
    in_sem, g_send, a_recv, b_recv, e_recv, h_recv, tb_recv, th_recv,
    first_send, r_send, r_recv, f_send, f_recv,
):
    rows, points = snapshots.shape
    size = rows // PARTS
    wide = rows // 2
    tm, space = lax.axis_index("tm"), lax.axis_index("space")
    core, y, x = tm % 2, (tm // 2) % 2, tm // 4
    z, half = space % NZ, space // NZ

    def device(x=x, y=y, core=core, half=half, z=z):
        return ((x * 2 + y) * 2 + core, half * NZ + z)

    x_next, x_last = (x + 1) % NX, (x + NX - 1) % NX
    twin = device(core=1 - core)
    beside = device(y=1 - y)
    x_up, x_down = device(x=x_next), device(x=x_last)
    z_up, z_down = device(z=(z + 1) % NZ), device(z=(z + NZ - 1) % NZ)
    far, far_up, far_down = device(half=1 - half), device(x=x_next, half=1 - half), device(x=x_last, half=1 - half)

    barrier = pltpu.get_barrier_semaphore()
    peers = (twin, beside, x_up, x_down, z_up, z_down, far, far_up, far_down)
    for peer in peers:
        pl.semaphore_signal(barrier, inc=1, device_id=peer, device_id_type=MESH)
    loads = [
        pltpu.make_async_copy(values_in, values, in_sem.at[0]),
        pltpu.make_async_copy(snapshots_in, snapshots, in_sem.at[1]),
    ]
    for load in loads:
        load.start()
    for load in loads:
        load.wait()

    tile_rows, tile_points = values.shape[2:]
    limit = threshold[0, 0]

    @pl.loop(0, points // tile_points)
    def _(c):
        lanes = pl.ds(pl.multiple_of(c * tile_points, tile_points), tile_points)
        for r in range(rows // tile_rows):
            across = pl.ds(r * tile_rows, tile_rows)
            dense = jnp.zeros((tile_rows, tile_points), jnp.float32)
            for k in range(values.shape[1]):
                listed = (cols[r, k] == c).astype(jnp.float32)
                dense = dense + listed * values[r, k].astype(jnp.float32)
            diff = snapshots[across, lanes].astype(jnp.float32) - dense
            shrunk = diff - jnp.clip(diff, -limit, limit)
            natural[across, lanes] = shrunk.astype(jnp.bfloat16)
            groups = shrunk.reshape(tile_rows // 32, PARTS, 8, tile_points)
            for n in range(PARTS):
                piece = groups[:, n].reshape(tile_rows // PARTS, tile_points)
                held[core, pl.ds(n * size + r * (tile_rows // PARTS), tile_rows // PARTS), lanes] = piece.astype(jnp.bfloat16)

    pl.semaphore_wait(barrier, len(peers))

    def remote(src, dst, send, recv, to):
        return pltpu.make_async_remote_copy(
            src_ref=src, dst_ref=dst, send_sem=send, recv_sem=recv, device_id=to, device_id_type=MESH
        )

    def portion(block, n):
        return held.at[block, pl.ds(n * (rows // PIECES), rows // PIECES)]

    a_copy = [remote(portion(core, n), portion(core, n), g_send, a_recv.at[n], twin) for n in range(PIECES)]
    b_copy = [remote(portion(core, n), portion(2 + core, n), g_send, b_recv.at[n], x_down) for n in range(PIECES)]
    e_copy = [
        remote(natural.at[pl.ds(q * wide, wide)], before.at[pl.ds(q * wide, wide)], g_send, e_recv.at[q], x_up)
        for q in range(2)
    ]
    h_from = core + 2 * (1 - y)
    h_copy = [remote(portion(h_from, n), portion(4 + core, n), g_send, h_recv.at[n], beside) for n in range(PIECES)]
    tb_copy = [remote(portion(2 + core, n), portion(2 + core, n), g_send, tb_recv.at[n], twin) for n in range(PIECES)]
    th_copy = [remote(portion(4 + core, n), portion(4 + core, n), g_send, th_recv.at[n], twin) for n in range(PIECES)]
    for copy in a_copy[:1] + b_copy[:1] + e_copy[:1] + a_copy[1:] + b_copy[1:] + e_copy[1:]:
        copy.start()

    def aa(n):
        return ("a", 0, (core, 1), (n * (1 + core), n * (1 + core) + core))

    def ab(n):
        return ("a", 4, (2, 3), (n, n))

    def ah(n):
        return ("a", 2, (4, 5), (n, n))

    def eh(q, n):
        return ("e", 6, (4, 5), (n, n), q)

    def eb(q, n):
        return ("e", 8, (2, 3), (n, n), q)

    def eb_last(q):
        return ("e", 8, (2, 2 + core), (core, 1), q)

    rounds = (
        ((aa(0),), (aa(1),)),
        ((ab(0),),),
        ((ab(1),), (ah(0),), (aa(2), eb(0, 0))),
        ((ab(2),), (ah(1),), (eh(0, 0),)),
        ((ab(3),), (ah(2),), (aa(3), eb(1, 0)), (eb_last(0),), (eb_last(1),), (eh(1, 0),)),
        ((eh(0, 1),), (eh(1, 1),), (ah(3),)),
    )
    units = [unit for group in rounds for unit in group]

    def each(place, action):
        if len(units[place]) == 1:
            action(units[place][0])
        else:
            for n, unit in enumerate(units[place]):
                @pl.when(core == n)
                def _(unit=unit):
                    action(unit)

    def rows_of(block, n, count):
        return held[block, pl.ds(pl.multiple_of(n * count, count), count), :]

    def times(left, right):
        return lax.dot_general(left, right, (((1,), (1,)), ((), ())), preferred_element_type=jnp.float32)

    def product(place):
        def action(unit):
            kind, _, blocks, parts = unit[:4]
            if kind == "a":
                left = jnp.concatenate([rows_of(b, n, size) for b, n in zip(blocks, parts)], axis=0)

                @pl.loop(0, 2)
                def _(q):
                    columns = pl.ds(pl.multiple_of(q * wide, wide), wide)
                    value = times(left, natural[columns, :]).reshape(2, 2, NZ, 8, wide)
                    for i in range(2):
                        part[place, :, :, pl.ds(8 * i, 8), columns] = value[i]
            else:
                q = unit[4]
                right = before[pl.ds(q * wide, wide), :]
                for i, (b, n) in enumerate(zip(blocks, parts)):
                    value = times(rows_of(b, n, 2 * size), right).reshape(2, 2, NZ, 8, wide)
                    for j in range(2):
                        part[place, :, :, pl.ds(8 * j, 8), pl.ds(i * wide, wide)] = value[j]

        each(place, action)

    ways = ((z_down, -1, 0), (z_up, 1, 1))

    def ring_copy(place, way, step):
        to, _, first = ways[way]
        src, dst = sent.at[place, way, step], got.at[place, way, step]
        if step == 0:
            src, dst = src.at[first], dst.at[first]
        return remote(src, dst, r_send if step else first_send, r_recv.at[place, way, step], to)

    def hop(place, way, step):
        _, sign, first = ways[way]
        goal = (z + NZ + sign * (4 - step)) % NZ
        if step > 0:
            ring_copy(place, way, step - 1).wait_recv()
        for h in range(2):
            if step == 0 and h != first:
                continue
            value = part[place, h, goal]
            if step > 1 or (step == 1 and h == first):
                value = value + got[place, way, step - 1, h].astype(jnp.float32)
            sent[place, way, step, h] = value.astype(jnp.bfloat16)
        ring_copy(place, way, step).start()

    def final_copies(place, unit):
        def copy(h, n, to):
            return remote(sum_out.at[place, h], sum_in.at[place, n], f_send, f_recv.at[place, n], to)

        if unit[0] == "a":
            return [copy(1 - half, 0, far)]
        return [copy(half, 0, x_down), copy(1 - half, 1, far_down)]

    def finish(place):
        for way in range(2):
            ring_copy(place, way, 3).wait_recv()
        for h in range(2):
            sum_out[place, h] = (
                part[place, h, z]
                + got[place, 0, 3, h].astype(jnp.float32)
                + got[place, 1, 3, h].astype(jnp.float32)
            )

        def action(unit):
            for copy in final_copies(place, unit):
                copy.start()

        each(place, action)

    def put(place):
        def action(unit):
            kind, base, blocks, parts = unit[:4]
            for copy in final_copies(place, unit):
                copy.wait_recv()
            if kind == "a":
                total = sum_out[place, half] + sum_in[place, 0]
            else:
                total = sum_in[place, 0] + sum_in[place, 1]
            for i, (b, n) in enumerate(zip(blocks, parts)):
                k = base + b % 2 - core
                if kind == "a":
                    out[k, pl.ds(pl.multiple_of(8 * n, 8), 8), :] = total[8 * i : 8 * i + 8]
                else:
                    q = unit[4]
                    out[k, pl.ds(pl.multiple_of(16 * n, 16), 16), pl.ds(q * wide, wide)] = total[:, i * wide : (i + 1) * wide]

        each(place, action)

    copies = {"a": a_copy, "b": tb_copy, "h": th_copy, "e": e_copy}
    waited = {kind: 0 for kind in copies}

    def need(kind, count):
        count *= 1 if kind == "e" else PIECES // PARTS
        for n in range(waited[kind], count):
            copies[kind][n].wait_recv()
        waited[kind] = max(waited[kind], count)

    for kind, n, *rest in plan():
        if kind == "b":
            b_copy[n].wait_recv()
            h_copy[n].start()
            tb_copy[n].start()
        elif kind == "h":
            h_copy[n].wait_recv()
            th_copy[n].start()
        elif kind == "unit":
            for what, count in NEEDS[n]:
                need(what, count)
            product(n)
            for way in range(2):
                hop(n, way, 0)
        elif kind == "hop":
            hop(n, *rest)
        elif kind == "sum":
            finish(n)
        else:
            put(n)

    remote(held, held, g_send, a_recv.at[0], twin).wait_send()
    steps = sent.at[:, :, pl.ds(1, 3)]
    remote(steps, steps, r_send, a_recv.at[0], twin).wait_send()
    firsts = sent.at[:, :, 0, 0]
    remote(firsts, firsts, first_send, a_recv.at[0], twin).wait_send()
    for n in range(2):
        count = sum(1 if unit[min(n, len(unit) - 1)][0] == "a" else 2 for unit in units)

        @pl.when(core == n)
        def _(count=count):
            sums = sum_out.at[pl.ds(0, count // 2)]
            remote(sums, sums, f_send, a_recv.at[0], twin).wait_send()


def local(snapshots, outlier_cols, outlier_values, threshold):
    rows, points = snapshots.shape
    scale = 1.0 / jnp.sqrt(jnp.float32(points * lax.axis_size("space")))
    dma = pltpu.SemaphoreType.DMA
    band = pl.pallas_call(
        kernel,
        out_shape=jax.ShapeDtypeStruct((9, 32, rows), jnp.float32),
        in_specs=[pl.BlockSpec(memory_space=pltpu.SMEM)] * 2 + [pl.BlockSpec(memory_space=pl.ANY)] * 2,
        out_specs=pl.BlockSpec(memory_space=pltpu.VMEM),
        scratch_shapes=[
            pltpu.VMEM(snapshots.shape, jnp.bfloat16),
            pltpu.VMEM(outlier_values.shape, jnp.bfloat16),
            pltpu.VMEM((6, rows, points), jnp.bfloat16),
            pltpu.VMEM((rows, points), jnp.bfloat16),
            pltpu.VMEM((rows, points), jnp.bfloat16),
            pltpu.VMEM((UNITS, 2, NZ, 16, rows), jnp.float32),
            pltpu.VMEM((UNITS, 2, 4, 2, 16, rows), jnp.bfloat16),
            pltpu.VMEM((UNITS, 2, 4, 2, 16, rows), jnp.bfloat16),
            pltpu.VMEM((UNITS, 2, 16, rows), jnp.float32),
            pltpu.VMEM((UNITS, 2, 16, rows), jnp.float32),
            dma((2,)),
            dma,
            *[dma((count,)) for count in (PIECES, PIECES, 2, PIECES, PIECES, PIECES)],
            dma,
            dma,
            dma((UNITS, 2, 4)),
            dma,
            dma((UNITS, 2)),
        ],
        compiler_params=pltpu.CompilerParams(
            collective_id=0, has_side_effects=True, vmem_limit_bytes=58 * 1024 * 1024
        ),
    )(outlier_cols, threshold.reshape(1, 1), snapshots, outlier_values)
    return jnp.transpose(band, (2, 0, 1)) * scale


def solution(mesh):
    placed = (P("tm", "space"), P("tm", "space"), P("tm", "space", None, None), P())
    return jax.shard_map(
        local, mesh=mesh, in_specs=placed, out_specs=P("tm", None, "space"), check_vma=False
    )
```

```python
import jax
import jax.numpy as jnp
from jax import lax
from jax.experimental import pallas as pl
from jax.experimental.pallas import tpu as pltpu
from jax.sharding import PartitionSpec as P

MESH = pl.DeviceIdType.MESH
NX, NZ = 4, 8
PARTS, PIECES = 4, 16
UNITS = 18


BOTH = {
    2: (("b", 1),), 3: (("b", 2),), 4: (("h", 1),), 6: (("b", 3),), 7: (("h", 2),), 8: (("h", 2), ("e", 1)),
    9: (("b", 4),), 10: (("h", 3),), 13: (("b", 4), ("e", 2)), 14: (("h", 2), ("e", 2)),
    15: (("b", 4), ("h", 4), ("e", 1)), 16: (("h", 4), ("e", 2)), 17: (("h", 4),),
}
NEEDS = (
    BOTH | {12: (("b", 2), ("h", 3), ("e", 1)), 0: (("a", 1),), 1: (("a", 2),), 5: (("a", 3),), 11: (("a", 4),)},
    BOTH | {12: (("b", 3), ("h", 3), ("e", 1)), 0: (), 1: (), 5: (("b", 2), ("e", 1)), 11: (("b", 2), ("e", 2))},
)


def plan(needs):
    rate, twin_rate, hop, twin_hop, multiply, add = 44.0, 220.0, 3.5, 2.0, 0.85, 0.15
    free, there, now, order = {}, {}, 0.0, []

    def send(link, size, latency=hop, speed=rate):
        free[link] = max(now, free.get(link, 0.0)) + size / speed
        return free[link] + latency

    piece = 2048 / PIECES
    for n in range(PIECES):
        there["a", n] = send("twin", piece, twin_hop, twin_rate)
        there["b", n] = send("down", piece)
    for n in range(2):
        there["e", n] = send("up", 1024)
    waiting = [(kind, n) for kind in "bh" for n in range(PIECES)]
    todo, flying = list(range(UNITS)), {}
    passed = {"a": "a", "b": "tb", "h": "th"}
    while todo or flying:
        choice = []
        for kind in "bh":
            left = [n for k, n in waiting if k == kind]
            if left and (kind, left[0]) in there:
                choice.append((there[kind, left[0]], 0, left[0], 0, (kind, left[0])))
        for unit in todo:
            keys = [
                (passed.get(k, k), n)
                for k, count in needs[unit]
                for n in range(count * (1 if k == "e" else PIECES // PARTS))
            ]
            if all(key in there for key in keys):
                choice.append((max((there[key] for key in keys), default=now), 2, unit, 0, ("unit", unit)))
        for unit, at in flying.items():
            for way in range(2):
                step = at[way]
                if step < 4:
                    choice.append((at[way, step - 1], 1, unit, step, ("hop", unit, way, step)))
            if "sum" in at:
                choice.append((at["sum"], 3, unit, 5, ("put", unit)))
            elif at[0] == at[1] == 4:
                choice.append((max(at[0, 3], at[1, 3]), 1, unit, 4, ("sum", unit)))
        now = max(now, min(c[0] for c in choice))
        action = min((c for c in choice if c[0] <= now), key=lambda c: c[1:4])[4]
        order.append(action)
        kind, n = action[:2]
        if kind == "b":
            waiting.remove(action)
            there["h", n] = send("beside", piece)
            there["tb", n] = send("twin", piece, twin_hop, twin_rate)
        elif kind == "h":
            waiting.remove(action)
            there["th", n] = send("twin", piece, twin_hop, twin_rate)
        elif kind == "unit":
            todo.remove(n)
            now += multiply + add
            flying[n] = {way: 1 for way in range(2)}
            for way in range(2):
                flying[n][way, 0] = send(way, 16)
        elif kind == "hop":
            way, step = action[2:]
            now += add
            flying[n][way, step] = send(way, 32)
            flying[n][way] = step + 1
        elif kind == "sum":
            now += add
            flying[n]["sum"] = send("far", 40, hop + 1.5)
        else:
            now += add
            del flying[n]
    return order


def kernel(
    cols, threshold, snapshots_in, values_in, out,
    snapshots, values, held, natural, before, part, sent, got, sum_out, sum_in,
    in_sem, g_send, a_recv, b_recv, e_recv, h_recv, tb_recv, th_recv,
    first_send, r_send, r_recv, f_send, f_recv,
):
    rows, points = snapshots.shape
    size = rows // PARTS
    wide = rows // 2
    tm, space = lax.axis_index("tm"), lax.axis_index("space")
    core, y, x = tm % 2, (tm // 2) % 2, tm // 4
    z, half = space % NZ, space // NZ

    def device(x=x, y=y, core=core, half=half, z=z):
        return ((x * 2 + y) * 2 + core, half * NZ + z)

    x_next, x_last = (x + 1) % NX, (x + NX - 1) % NX
    twin = device(core=1 - core)
    beside = device(y=1 - y)
    x_up, x_down = device(x=x_next), device(x=x_last)
    z_up, z_down = device(z=(z + 1) % NZ), device(z=(z + NZ - 1) % NZ)
    far, far_up, far_down = device(half=1 - half), device(x=x_next, half=1 - half), device(x=x_last, half=1 - half)

    barrier = pltpu.get_barrier_semaphore()
    peers = (twin, beside, x_up, x_down, z_up, z_down, far, far_up, far_down)
    for peer in peers:
        pl.semaphore_signal(barrier, inc=1, device_id=peer, device_id_type=MESH)
    loads = [
        pltpu.make_async_copy(values_in, values, in_sem.at[0]),
        pltpu.make_async_copy(snapshots_in, snapshots, in_sem.at[1]),
    ]
    for load in loads:
        load.start()
    for load in loads:
        load.wait()

    tile_rows, tile_points = values.shape[2:]
    limit = threshold[0, 0]

    @pl.loop(0, points // tile_points)
    def _(c):
        lanes = pl.ds(pl.multiple_of(c * tile_points, tile_points), tile_points)
        for r in range(rows // tile_rows):
            across = pl.ds(r * tile_rows, tile_rows)
            dense = jnp.zeros((tile_rows, tile_points), jnp.float32)
            for k in range(values.shape[1]):
                listed = (cols[r, k] == c).astype(jnp.float32)
                dense = dense + listed * values[r, k].astype(jnp.float32)
            diff = snapshots[across, lanes].astype(jnp.float32) - dense
            shrunk = diff - jnp.clip(diff, -limit, limit)
            natural[across, lanes] = shrunk.astype(jnp.bfloat16)
            groups = shrunk.reshape(tile_rows // 32, PARTS, 8, tile_points)
            for n in range(PARTS):
                piece = groups[:, n].reshape(tile_rows // PARTS, tile_points)
                held[core, pl.ds(n * size + r * (tile_rows // PARTS), tile_rows // PARTS), lanes] = piece.astype(jnp.bfloat16)

    pl.semaphore_wait(barrier, len(peers))

    def remote(src, dst, send, recv, to):
        return pltpu.make_async_remote_copy(
            src_ref=src, dst_ref=dst, send_sem=send, recv_sem=recv, device_id=to, device_id_type=MESH
        )

    def portion(block, n):
        return held.at[block, pl.ds(n * (rows // PIECES), rows // PIECES)]

    a_copy = [remote(portion(core, n), portion(core, n), g_send, a_recv.at[n], twin) for n in range(PIECES)]
    b_copy = [remote(portion(core, n), portion(2 + core, n), g_send, b_recv.at[n], x_down) for n in range(PIECES)]
    e_copy = [
        remote(natural.at[pl.ds(q * wide, wide)], before.at[pl.ds(q * wide, wide)], g_send, e_recv.at[q], x_up)
        for q in range(2)
    ]
    h_from = core + 2 * (1 - y)
    h_copy = [remote(portion(h_from, n), portion(4 + core, n), g_send, h_recv.at[n], beside) for n in range(PIECES)]
    tb_copy = [remote(portion(2 + core, n), portion(2 + core, n), g_send, tb_recv.at[n], twin) for n in range(PIECES)]
    th_copy = [remote(portion(4 + core, n), portion(4 + core, n), g_send, th_recv.at[n], twin) for n in range(PIECES)]
    for copy in a_copy[:1] + b_copy[:1] + e_copy[:1] + a_copy[1:] + b_copy[1:] + e_copy[1:]:
        copy.start()

    def aa(n):
        return ("a", 0, (core, 1), (n * (1 + core), n * (1 + core) + core))

    def ab(n):
        return ("a", 4, (2, 3), (n, n))

    def ah(n):
        return ("a", 2, (4, 5), (n, n))

    def eh(q, n):
        return ("e", 0, (4, 4, 5, 5), (2 * n, 2 * n + 1) * 2, q)

    def eb(q, n):
        return ("e", 0, (2, 2, 3, 3), (2 * n, 2 * n + 1) * 2, q)

    def eb_all(q):
        return ("e", 0, (2, 2, 2, 2), (0, 1, 2, 3), q)

    def e_mixed(n):
        return ("e", 0, (2, 2, 4, 5), (2 * n - 4, 2 * n - 3, n, n), 0)

    def e_part(n):
        return ("e", 0, (2, 3, 4, 5), (n, n, n, n), 0)

    rounds = (
        ((aa(0),), (aa(1),)),
        ((ab(0),),),
        ((ab(1),), (ah(0),), (aa(2), eb(0, 0))),
        ((ab(2),), (ah(1),), (eh(0, 0),)),
        ((ab(3),), (ah(2),), (aa(3), eb(1, 0)), (e_mixed(2), e_part(2)), (eb_all(1), eb(1, 1)), (eh(1, 0),)),
        ((e_mixed(3), e_part(3)), (eh(1, 1),), (ah(3),)),
    )
    units = [unit for group in rounds for unit in group]

    side = [0]

    def each(place, action):
        action(units[place][min(side[0], len(units[place]) - 1)])

    def rows_of(block, n, count):
        return held[block, pl.ds(pl.multiple_of(n * count, count), count), :]

    def times(left, right):
        return lax.dot_general(left, right, (((1,), (1,)), ((), ())), preferred_element_type=jnp.float32)

    def product(place):
        def action(unit):
            kind, _, blocks, parts = unit[:4]
            if kind == "a":
                left = jnp.concatenate([rows_of(b, n, size) for b, n in zip(blocks, parts)], axis=0)

                @pl.loop(0, 2)
                def _(q):
                    columns = pl.ds(pl.multiple_of(q * wide, wide), wide)
                    value = times(left, natural[columns, :]).reshape(2, 2, NZ, 8, wide)
                    for i in range(2):
                        part[place, :, :, pl.ds(8 * i, 8), columns] = value[i]
            else:
                q = unit[4]
                right = before[pl.ds(q * wide, wide), :]
                for i in range(2):
                    chosen = list(zip(blocks, parts))[2 * i : 2 * i + 2]
                    left = jnp.concatenate([rows_of(b, n, size) for b, n in chosen], axis=0)
                    value = times(left, right).reshape(2, 2, NZ, 8, wide)
                    for j in range(2):
                        part[place, :, :, pl.ds(8 * j, 8), pl.ds(i * wide, wide)] = value[j]

        each(place, action)

    ways = ((z_down, -1, 0), (z_up, 1, 1))

    def ring_copy(place, way, step):
        to, _, first = ways[way]
        src, dst = sent.at[place, way, step], got.at[place, way, step]
        if step == 0:
            src, dst = src.at[first], dst.at[first]
        return remote(src, dst, r_send if step else first_send, r_recv.at[place, way, step], to)

    def hop(place, way, step):
        _, sign, first = ways[way]
        goal = (z + NZ + sign * (4 - step)) % NZ
        if step > 0:
            ring_copy(place, way, step - 1).wait_recv()
        for h in range(2):
            if step == 0 and h != first:
                continue
            value = part[place, h, goal]
            if step > 1 or (step == 1 and h == first):
                value = value + got[place, way, step - 1, h].astype(jnp.float32)
            sent[place, way, step, h] = value.astype(jnp.bfloat16)
        ring_copy(place, way, step).start()

    def final_copies(place, unit):
        def copy(h, n, to):
            return remote(sum_out.at[place, h], sum_in.at[place, n], f_send, f_recv.at[place, n], to)

        if unit[0] == "a":
            return [copy(1 - half, 0, far)]
        return [copy(half, 0, x_down), copy(1 - half, 1, far_down)]

    def finish(place):
        for way in range(2):
            ring_copy(place, way, 3).wait_recv()
        for h in range(2):
            sum_out[place, h] = (
                part[place, h, z]
                + got[place, 0, 3, h].astype(jnp.float32)
                + got[place, 1, 3, h].astype(jnp.float32)
            )

        def action(unit):
            for copy in final_copies(place, unit):
                copy.start()

        each(place, action)

    def put(place):
        def action(unit):
            kind, base, blocks, parts = unit[:4]
            for copy in final_copies(place, unit):
                copy.wait_recv()
            if kind == "a":
                total = sum_out[place, half] + sum_in[place, 0]
            else:
                total = sum_in[place, 0] + sum_in[place, 1]
            for i, (b, n) in enumerate(zip(blocks, parts)):
                if kind == "a":
                    out[base + b % 2 - core, pl.ds(pl.multiple_of(8 * n, 8), 8), :] = total[8 * i : 8 * i + 8]
                else:
                    q, away = unit[4], 8 if b < 4 else 6
                    up, over = 8 * (i % 2), wide * (i // 2)
                    out[away + b % 2 - core, pl.ds(8 * n, 8), pl.ds(q * wide, wide)] = total[up : up + 8, over : over + wide]

        each(place, action)

    copies = {"a": a_copy, "b": tb_copy, "h": th_copy, "e": e_copy}

    def run(needs):
        waited = {kind: 0 for kind in copies}

        def need(kind, count):
            count *= 1 if kind == "e" else PIECES // PARTS
            for n in range(waited[kind], count):
                copies[kind][n].wait_recv()
            waited[kind] = max(waited[kind], count)

        for kind, n, *rest in plan(needs):
            if kind == "b":
                b_copy[n].wait_recv()
                h_copy[n].start()
                tb_copy[n].start()
            elif kind == "h":
                h_copy[n].wait_recv()
                th_copy[n].start()
            elif kind == "unit":
                for what, count in needs[n]:
                    need(what, count)
                product(n)
                for way in range(2):
                    hop(n, way, 0)
            elif kind == "hop":
                hop(n, *rest)
            elif kind == "sum":
                finish(n)
            else:
                put(n)
        for what, count in (("a", PARTS), ("b", PARTS), ("h", PARTS), ("e", 2)):
            need(what, count)

    for n in range(2):
        @pl.when(core == n)
        def _(n=n):
            side[0] = n
            run(NEEDS[n])

    remote(held, held, g_send, a_recv.at[0], twin).wait_send()
    steps = sent.at[:, :, pl.ds(1, 3)]
    remote(steps, steps, r_send, a_recv.at[0], twin).wait_send()
    firsts = sent.at[:, :, 0, 0]
    remote(firsts, firsts, first_send, a_recv.at[0], twin).wait_send()
    for n in range(2):
        count = sum(1 if unit[min(n, len(unit) - 1)][0] == "a" else 2 for unit in units)

        @pl.when(core == n)
        def _(count=count):
            sums = sum_out.at[pl.ds(0, count // 2)]
            remote(sums, sums, f_send, a_recv.at[0], twin).wait_send()


def local(snapshots, outlier_cols, outlier_values, threshold):
    rows, points = snapshots.shape
    scale = 1.0 / jnp.sqrt(jnp.float32(points * lax.axis_size("space")))
    dma = pltpu.SemaphoreType.DMA
    band = pl.pallas_call(
        kernel,
        out_shape=jax.ShapeDtypeStruct((9, 32, rows), jnp.float32),
        in_specs=[pl.BlockSpec(memory_space=pltpu.SMEM)] * 2 + [pl.BlockSpec(memory_space=pl.ANY)] * 2,
        out_specs=pl.BlockSpec(memory_space=pltpu.VMEM),
        scratch_shapes=[
            pltpu.VMEM(snapshots.shape, jnp.bfloat16),
            pltpu.VMEM(outlier_values.shape, jnp.bfloat16),
            pltpu.VMEM((6, rows, points), jnp.bfloat16),
            pltpu.VMEM((rows, points), jnp.bfloat16),
            pltpu.VMEM((rows, points), jnp.bfloat16),
            pltpu.VMEM((UNITS, 2, NZ, 16, rows), jnp.float32),
            pltpu.VMEM((UNITS, 2, 4, 2, 16, rows), jnp.bfloat16),
            pltpu.VMEM((UNITS, 2, 4, 2, 16, rows), jnp.bfloat16),
            pltpu.VMEM((UNITS, 2, 16, rows), jnp.float32),
            pltpu.VMEM((UNITS, 2, 16, rows), jnp.float32),
            dma((2,)),
            dma,
            *[dma((count,)) for count in (PIECES, PIECES, 2, PIECES, PIECES, PIECES)],
            dma,
            dma,
            dma((UNITS, 2, 4)),
            dma,
            dma((UNITS, 2)),
        ],
        compiler_params=pltpu.CompilerParams(
            collective_id=0, has_side_effects=True, vmem_limit_bytes=58 * 1024 * 1024
        ),
    )(outlier_cols, threshold.reshape(1, 1), snapshots, outlier_values)
    return jnp.transpose(band, (2, 0, 1)) * scale


def solution(mesh):
    placed = (P("tm", "space"), P("tm", "space"), P("tm", "space", None, None), P())
    return jax.shard_map(
        local, mesh=mesh, in_specs=placed, out_specs=P("tm", None, "space"), check_vma=False
    )
```

```python
import jax
import jax.numpy as jnp
from jax import lax
from jax.experimental import pallas as pl
from jax.experimental.pallas import tpu as pltpu
from jax.sharding import PartitionSpec as P

MESH = pl.DeviceIdType.MESH
NX, NZ = 4, 8
PARTS, PIECES = 4, 16
UNITS = 18

NEEDS = (
    (("a", 1),), (("a", 2),),
    (("b", 1),),
    (("b", 2),), (("h", 1),), (("a", 3), ("b", 2), ("e", 1)),
    (("b", 3),), (("h", 2),), (("h", 2), ("e", 1)),
    (("b", 4),), (("h", 3),), (("a", 4), ("b", 2), ("e", 2)),
    (("b", 4), ("e", 1)), (("b", 4), ("e", 2)), (("h", 2), ("e", 2)),
    (("h", 4), ("e", 1)), (("h", 4), ("e", 2)), (("h", 4),),
)


def plan():
    rate, twin_rate, hop, twin_hop, multiply, add = 44.0, 220.0, 3.5, 2.0, 0.85, 0.15
    free, there, now, order = {}, {}, 0.0, []

    def send(link, size, latency=hop, speed=rate):
        free[link] = max(now, free.get(link, 0.0)) + size / speed
        return free[link] + latency

    piece = 2048 / PIECES
    for n in range(PIECES):
        there["a", n] = send("twin", piece, twin_hop, twin_rate)
        there["b", n] = send("down", piece)
    for n in range(2):
        there["e", n] = send("up", 1024)
    waiting = [(kind, n) for kind in "bh" for n in range(PIECES)]
    todo, flying = list(range(UNITS)), {}
    passed = {"a": "a", "b": "tb", "h": "th"}
    while todo or flying:
        choice = []
        for kind in "bh":
            left = [n for k, n in waiting if k == kind]
            if left and (kind, left[0]) in there:
                choice.append((there[kind, left[0]], 0, left[0], 0, (kind, left[0])))
        for unit in todo:
            keys = [
                (passed.get(k, k), n)
                for k, count in NEEDS[unit]
                for n in range(count * (1 if k == "e" else PIECES // PARTS))
            ]
            if all(key in there for key in keys):
                choice.append((max(there[key] for key in keys), 2, unit, 0, ("unit", unit)))
        for unit, at in flying.items():
            for way in range(2):
                step = at[way]
                if step < 4:
                    choice.append((at[way, step - 1], 1, unit, step, ("hop", unit, way, step)))
            if "sum" in at:
                choice.append((at["sum"], 3, unit, 5, ("put", unit)))
            elif at[0] == at[1] == 4:
                choice.append((max(at[0, 3], at[1, 3]), 1, unit, 4, ("sum", unit)))
        now = max(now, min(c[0] for c in choice))
        action = min((c for c in choice if c[0] <= now), key=lambda c: c[1:4])[4]
        order.append(action)
        kind, n = action[:2]
        if kind == "b":
            waiting.remove(action)
            there["h", n] = send("beside", piece)
            there["tb", n] = send("twin", piece, twin_hop, twin_rate)
        elif kind == "h":
            waiting.remove(action)
            there["th", n] = send("twin", piece, twin_hop, twin_rate)
        elif kind == "unit":
            todo.remove(n)
            now += multiply + add
            flying[n] = {way: 1 for way in range(2)}
            for way in range(2):
                flying[n][way, 0] = send(way, 16)
        elif kind == "hop":
            way, step = action[2:]
            now += add
            flying[n][way, step] = send(way, 32)
            flying[n][way] = step + 1
        elif kind == "sum":
            now += add
            flying[n]["sum"] = send("far", 40, hop + 1.5)
        else:
            now += add
            del flying[n]
    return order


def kernel(
    cols, threshold, snapshots_in, values_in, out,
    snapshots, values, held, natural, before, part, sent, got, sum_out, sum_in,
    in_sem, g_send, a_recv, b_recv, e_recv, h_recv, tb_recv, th_recv,
    first_send, r_send, r_recv, f_send, f_recv,
):
    rows, points = snapshots.shape
    size = rows // PARTS
    wide = rows // 2
    tm, space = lax.axis_index("tm"), lax.axis_index("space")
    core, y, x = tm % 2, (tm // 2) % 2, tm // 4
    z, half = space % NZ, space // NZ

    def device(x=x, y=y, core=core, half=half, z=z):
        return ((x * 2 + y) * 2 + core, half * NZ + z)

    x_next, x_last = (x + 1) % NX, (x + NX - 1) % NX
    twin = device(core=1 - core)
    beside = device(y=1 - y)
    x_up, x_down = device(x=x_next), device(x=x_last)
    z_up, z_down = device(z=(z + 1) % NZ), device(z=(z + NZ - 1) % NZ)
    far, far_up, far_down = device(half=1 - half), device(x=x_next, half=1 - half), device(x=x_last, half=1 - half)

    barrier = pltpu.get_barrier_semaphore()
    peers = (twin, beside, x_up, x_down, z_up, z_down, far, far_up, far_down)
    for peer in peers:
        pl.semaphore_signal(barrier, inc=1, device_id=peer, device_id_type=MESH)
    loads = [
        pltpu.make_async_copy(values_in, values, in_sem.at[0]),
        pltpu.make_async_copy(snapshots_in, snapshots, in_sem.at[1]),
    ]
    for load in loads:
        load.start()
    for load in loads:
        load.wait()

    tile_rows, tile_points = values.shape[2:]
    limit = threshold[0, 0]

    @pl.loop(0, points // tile_points)
    def _(c):
        lanes = pl.ds(pl.multiple_of(c * tile_points, tile_points), tile_points)
        for r in range(rows // tile_rows):
            across = pl.ds(r * tile_rows, tile_rows)
            dense = jnp.zeros((tile_rows, tile_points), jnp.float32)
            for k in range(values.shape[1]):
                listed = (cols[r, k] == c).astype(jnp.float32)
                dense = dense + listed * values[r, k].astype(jnp.float32)
            diff = snapshots[across, lanes].astype(jnp.float32) - dense
            shrunk = diff - jnp.clip(diff, -limit, limit)
            natural[across, lanes] = shrunk.astype(jnp.bfloat16)
            groups = shrunk.reshape(tile_rows // 32, PARTS, 8, tile_points)
            for n in range(PARTS):
                piece = groups[:, n].reshape(tile_rows // PARTS, tile_points)
                held[core, pl.ds(n * size + r * (tile_rows // PARTS), tile_rows // PARTS), lanes] = piece.astype(jnp.bfloat16)

    pl.semaphore_wait(barrier, len(peers))

    def remote(src, dst, send, recv, to):
        return pltpu.make_async_remote_copy(
            src_ref=src, dst_ref=dst, send_sem=send, recv_sem=recv, device_id=to, device_id_type=MESH
        )

    def portion(block, n):
        return held.at[block, pl.ds(n * (rows // PIECES), rows // PIECES)]

    quarters = [held.at[core, pl.ds(n * size, size)] for n in range(PARTS)]
    a_copy = [remote(quarter, quarter, g_send, a_recv.at[n], twin) for n, quarter in enumerate(quarters)]
    b_copy = [remote(portion(core, n), portion(2 + core, n), g_send, b_recv.at[n], x_down) for n in range(PIECES)]
    e_copy = [
        remote(natural.at[pl.ds(q * wide, wide)], before.at[pl.ds(q * wide, wide)], g_send, e_recv.at[q], x_up)
        for q in range(2)
    ]
    h_from = core + 2 * (1 - y)
    h_copy = [remote(portion(h_from, n), portion(4 + core, n), g_send, h_recv.at[n], beside) for n in range(PIECES)]
    tb_copy = [remote(portion(2 + core, n), portion(2 + core, n), g_send, tb_recv.at[n], twin) for n in range(PIECES)]
    th_copy = [remote(portion(4 + core, n), portion(4 + core, n), g_send, th_recv.at[n], twin) for n in range(PIECES)]
    for copy in a_copy[:1] + b_copy[:1] + e_copy[:1] + a_copy[1:] + b_copy[1:] + e_copy[1:]:
        copy.start()

    def aa(n):
        return ("a", 0, (core, 1), (n * (1 + core), n * (1 + core) + core))

    def ab(n):
        return ("a", 4, (2, 3), (n, n))

    def ah(n):
        return ("a", 2, (4, 5), (n, n))

    def eh(q, n):
        return ("e", 6, (4, 5), (n, n), q)

    def eb(q, n):
        return ("e", 8, (2, 3), (n, n), q)

    def eb_last(q):
        return ("e", 8, (2, 2 + core), (core, 1), q)

    rounds = (
        ((aa(0),), (aa(1),)),
        ((ab(0),),),
        ((ab(1),), (ah(0),), (aa(2), eb(0, 0))),
        ((ab(2),), (ah(1),), (eh(0, 0),)),
        ((ab(3),), (ah(2),), (aa(3), eb(1, 0)), (eb_last(0),), (eb_last(1),), (eh(1, 0),)),
        ((eh(0, 1),), (eh(1, 1),), (ah(3),)),
    )
    units = [unit for group in rounds for unit in group]

    def each(place, action):
        if len(units[place]) == 1:
            action(units[place][0])
        else:
            for n, unit in enumerate(units[place]):
                @pl.when(core == n)
                def _(unit=unit):
                    action(unit)

    def rows_of(block, n, count):
        return held[block, pl.ds(pl.multiple_of(n * count, count), count), :]

    def times(left, right):
        return lax.dot_general(left, right, (((1,), (1,)), ((), ())), preferred_element_type=jnp.float32)

    def product(place):
        def action(unit):
            kind, _, blocks, parts = unit[:4]
            if kind == "a":
                left = jnp.concatenate([rows_of(b, n, size) for b, n in zip(blocks, parts)], axis=0)

                value = times(left, natural[...]).reshape(2, 2, NZ, 8, rows)
                for i in range(2):
                    part[place, :, :, pl.ds(8 * i, 8), :] = value[i]
            else:
                q = unit[4]
                right = before[pl.ds(q * wide, wide), :]
                for i, (b, n) in enumerate(zip(blocks, parts)):
                    value = times(rows_of(b, n, 2 * size), right).reshape(2, 2, NZ, 8, wide)
                    for j in range(2):
                        part[place, :, :, pl.ds(8 * j, 8), pl.ds(i * wide, wide)] = value[j]

        each(place, action)

    ways = ((z_down, -1, 0), (z_up, 1, 1))

    def ring_copy(place, way, step):
        to, _, first = ways[way]
        src, dst = sent.at[place, way, step], got.at[place, way, step]
        if step == 0:
            src, dst = src.at[first], dst.at[first]
        return remote(src, dst, r_send if step else first_send, r_recv.at[place, way, step], to)

    def hop(place, way, step):
        _, sign, first = ways[way]
        goal = (z + NZ + sign * (4 - step)) % NZ
        if step > 0:
            ring_copy(place, way, step - 1).wait_recv()
        for h in range(2):
            if step == 0 and h != first:
                continue
            value = part[place, h, goal]
            if step > 1 or (step == 1 and h == first):
                value = value + got[place, way, step - 1, h].astype(jnp.float32)
            sent[place, way, step, h] = value.astype(jnp.bfloat16)
        ring_copy(place, way, step).start()

    def final_copies(place, unit):
        def copy(h, n, to):
            return remote(sum_out.at[place, h], sum_in.at[place, n], f_send, f_recv.at[place, n], to)

        if unit[0] == "a":
            return [copy(1 - half, 0, far)]
        return [copy(half, 0, x_down), copy(1 - half, 1, far_down)]

    def finish(place):
        for way in range(2):
            ring_copy(place, way, 3).wait_recv()
        for h in range(2):
            sum_out[place, h] = (
                part[place, h, z]
                + got[place, 0, 3, h].astype(jnp.float32)
                + got[place, 1, 3, h].astype(jnp.float32)
            )

        def action(unit):
            for copy in final_copies(place, unit):
                copy.start()

        each(place, action)

    def put(place):
        def action(unit):
            kind, base, blocks, parts = unit[:4]
            for copy in final_copies(place, unit):
                copy.wait_recv()
            if kind == "a":
                total = sum_out[place, half] + sum_in[place, 0]
            else:
                total = sum_in[place, 0] + sum_in[place, 1]
            for i, (b, n) in enumerate(zip(blocks, parts)):
                k = base + b % 2 - core
                if kind == "a":
                    out[k, pl.ds(pl.multiple_of(8 * n, 8), 8), :] = total[8 * i : 8 * i + 8]
                else:
                    q = unit[4]
                    out[k, pl.ds(pl.multiple_of(16 * n, 16), 16), pl.ds(q * wide, wide)] = total[:, i * wide : (i + 1) * wide]

        each(place, action)

    copies = {"a": a_copy, "b": tb_copy, "h": th_copy, "e": e_copy}
    waited = {kind: 0 for kind in copies}

    def need(kind, count):
        count *= 1 if kind in "ae" else PIECES // PARTS
        for n in range(waited[kind], count):
            copies[kind][n].wait_recv()
        waited[kind] = max(waited[kind], count)

    for kind, n, *rest in plan():
        if kind == "b":
            b_copy[n].wait_recv()
            h_copy[n].start()
            tb_copy[n].start()
        elif kind == "h":
            h_copy[n].wait_recv()
            th_copy[n].start()
        elif kind == "unit":
            for what, count in NEEDS[n]:
                need(what, count)
            product(n)
            for way in range(2):
                hop(n, way, 0)
        elif kind == "hop":
            hop(n, *rest)
        elif kind == "sum":
            finish(n)
        else:
            put(n)

    remote(held, held, g_send, a_recv.at[0], twin).wait_send()
    steps = sent.at[:, :, pl.ds(1, 3)]
    remote(steps, steps, r_send, a_recv.at[0], twin).wait_send()
    firsts = sent.at[:, :, 0, 0]
    remote(firsts, firsts, first_send, a_recv.at[0], twin).wait_send()
    for n in range(2):
        count = sum(1 if unit[min(n, len(unit) - 1)][0] == "a" else 2 for unit in units)

        @pl.when(core == n)
        def _(count=count):
            sums = sum_out.at[pl.ds(0, count // 2)]
            remote(sums, sums, f_send, a_recv.at[0], twin).wait_send()


def local(snapshots, outlier_cols, outlier_values, threshold):
    rows, points = snapshots.shape
    scale = 1.0 / jnp.sqrt(jnp.float32(points * lax.axis_size("space")))
    dma = pltpu.SemaphoreType.DMA
    band = pl.pallas_call(
        kernel,
        out_shape=jax.ShapeDtypeStruct((9, 32, rows), jnp.float32),
        in_specs=[pl.BlockSpec(memory_space=pltpu.SMEM)] * 2 + [pl.BlockSpec(memory_space=pl.ANY)] * 2,
        out_specs=pl.BlockSpec(memory_space=pltpu.VMEM),
        scratch_shapes=[
            pltpu.VMEM(snapshots.shape, jnp.bfloat16),
            pltpu.VMEM(outlier_values.shape, jnp.bfloat16),
            pltpu.VMEM((6, rows, points), jnp.bfloat16),
            pltpu.VMEM((rows, points), jnp.bfloat16),
            pltpu.VMEM((rows, points), jnp.bfloat16),
            pltpu.VMEM((UNITS, 2, NZ, 16, rows), jnp.float32),
            pltpu.VMEM((UNITS, 2, 4, 2, 16, rows), jnp.bfloat16),
            pltpu.VMEM((UNITS, 2, 4, 2, 16, rows), jnp.bfloat16),
            pltpu.VMEM((UNITS, 2, 16, rows), jnp.float32),
            pltpu.VMEM((UNITS, 2, 16, rows), jnp.float32),
            dma((2,)),
            dma,
            *[dma((count,)) for count in (PARTS, PIECES, 2, PIECES, PIECES, PIECES)],
            dma,
            dma,
            dma((UNITS, 2, 4)),
            dma,
            dma((UNITS, 2)),
        ],
        compiler_params=pltpu.CompilerParams(
            collective_id=0, has_side_effects=True, vmem_limit_bytes=58 * 1024 * 1024
        ),
    )(outlier_cols, threshold.reshape(1, 1), snapshots, outlier_values)
    return jnp.transpose(band, (2, 0, 1)) * scale


def solution(mesh):
    placed = (P("tm", "space"), P("tm", "space"), P("tm", "space", None, None), P())
    return jax.shard_map(
        local, mesh=mesh, in_specs=placed, out_specs=P("tm", None, "space"), check_vma=False
    )
```
